128 devices in a mesh: seq: 32 (over y, x, core), tp: 4 (over z).
Axes of the slice: x: 4, y: 4, z: 4, core: 2. Of those that a mesh axis runs over, the one named last changes fastest.
Arguments:
- tokens: bfloat16 [8192, 1536], P('seq'), may hold values from -6 to 6
- doc_ids: int32 [8192], P('seq'), may hold values from 0 to 3, never falling along the last dimension, each value on 1 to 4096 neighbouring positions
- mix_gain: bfloat16 [1536], replicated, may hold values from 0.25 to 1.75
- zgate_proj: bfloat16 [1536, 3072], P(None, 'tp'), may hold values from -0.15625 to 0.15625
- xin_proj: bfloat16 [1536, 3072], P(None, 'tp'), may hold values from -0.15625 to 0.15625
- bc_proj: bfloat16 [1536, 256], replicated, may hold values from -0.15625 to 0.15625
- dt_proj: bfloat16 [1536, 48], P(None, 'tp'), may hold values from -0.15625 to 0.15625
- conv_x: bfloat16 [4, 3072], P(None, 'tp'), may hold values from -3 to 3
- conv_bc: bfloat16 [4, 256], replicated, may hold values from -3 to 3
- dt_bias: float32 [48], P('tp'), may hold values from -3 to -1
- decay_rate: float32 [48], P('tp'), may hold values from 0.0001 to 0.5
- skip_gain: float32 [48], P('tp'), may hold values from 1 to 16
- norm_gain: bfloat16 [3072], P('tp'), may hold values from 0.25 to 1.75
- out_proj: bfloat16 [3072, 1536], P('tp'), may hold values from -0.109375 to 0.109375
- moe_gain: bfloat16 [1536], replicated, may hold values from 0.25 to 1.75
- router: bfloat16 [1536, 64], replicated, may hold values from -0.15625 to 0.15625
- routes: int32 [8192, 6], P('seq'), may hold values from 0 to 63, all different within a row; in each aligned block of 256 rows (0 to 255, 256 to 511, ...) at most 48 rows name the same one
- expert_gate_up: bfloat16 [64, 2, 1536, 512], P('seq', None, None, 'tp'), may hold values from -0.15625 to 0.15625
- expert_down: bfloat16 [64, 512, 1536], P('seq', 'tp'), may hold values from -0.25 to 0.25
- shared_gate_up: bfloat16 [2, 1536, 1024], P(None, None, 'tp'), may hold values from -0.15625 to 0.15625
- shared_down: bfloat16 [1024, 1536], P('tp'), may hold values from -0.1875 to 0.1875
Outputs:
- mixed: bfloat16 [8192, 1536], P('seq', 'tp')
The draws below stay inside these ranges and needn't reach their ends.
Inputs may be any that keep to these rules, and one draw needn't show every extreme that they name: `doc_ids`: Non-decreasing along the tokens; each prompt holds 1 to 4096 tokens, one exactly 4096. `routes`: in each aligned block of 256 rows (the rows of one index of seq) no expert is named by more than 48 rows, a bound that some block reaches.
All inputs are finite; a program needn't handle non-finite values.
Results may differ from the reference program's by a relative error of at most 0.013.
Values may be sent and summed in bfloat16 or wider, within the bound.
A program may use at most 128 MiB of HBM per device.

```python
import math
import jax
import jax.numpy as jnp
import numpy as np
from jax import lax

D = 1536
HEADS = 48
HEAD = 64
NSTATE = 128
KCONV = 4
FFE = 512
FFS = 1024
TOP = 6
DOCS = 4
TOK_DEV = 256
EXPERTS = 64
DI = 3072
TOKENS = 8192
CAP = 48
FFQ = 128
N_SEQ = 32
N_TP = 4


def levels(stream_key, shape, cuts, least, high):
    def one(position, blocks):
        steps = jax.random.uniform(jax.random.fold_in(jax.random.fold_in(stream_key, 6), position), (blocks,), jnp.float32, least / len(cuts), high / len(cuts))
        return jnp.repeat(jnp.exp(steps), shape[position] // blocks).reshape((-1,) + (1,) * (len(shape) - position - 1))

    factor_of = one(*cuts[0])
    for cut in cuts[1:]:
        factor_of = factor_of * one(*cut)
    return factor_of


def length_profile(count, total, limit, skew):
    loads = [(1 << 20) // math.isqrt(rank ** skew) + 1 for rank in range(2, count + 1)]
    surplus, counts = total - limit - (count - 1), [1] * (count - 1)
    while surplus > 0:
        movable = [i for i in range(count - 1) if counts[i] < limit]
        pool, remaining = sum([loads[i] for i in movable]), surplus
        for i in movable:
            extra = min(limit - counts[i], max(1, remaining * loads[i] // pool), surplus)
            counts[i] = counts[i] + extra
            surplus = surplus - extra
    return np.array([limit] + counts)


def uneven(own_key, amount, total, most, lean):
    if amount == 2:
        one = jax.random.randint(own_key, (), max(1, total - most), min(most, total - 1) + 1)
        return jnp.stack([one, total - one])
    sizes = jnp.asarray(length_profile(amount, total, most, lean), jnp.int32)
    couples = (amount - 1) // 2
    donor, receiver = sizes[1:1 + 2 * couples:2], sizes[2:2 + 2 * couples:2]
    margin = jnp.minimum(donor - 1, most - receiver)
    passed = jax.random.randint(jax.random.fold_in(own_key, 1), (couples,), 0, 1 << 20) % (margin + 1)
    sizes = sizes.at[1:1 + 2 * couples:2].set(donor - passed).at[2:2 + 2 * couples:2].set(receiver + passed)
    return sizes[jax.random.permutation(jax.random.fold_in(own_key, 2), amount)]


def routed_block(own_key, own, number, rows, count, top, bound, skew):
    sequence = jax.random.permutation(own_key, count)
    heavy_load, usual = shares(count, rows * top, bound, skew, True), shares(count, rows * top, bound, skew, False)
    places = jnp.arange(count)

    def named(sizes, rotation):
        used = int((sizes > 0).sum())
        fixed = max(1, used // 4)
        moved = fixed + (places - fixed + rotation * (used - fixed)) % max(1, count - fixed)
        return jnp.zeros((count,), jnp.int32).at[sequence[jnp.where(places < fixed, places, moved)]].set(jnp.asarray(sizes, jnp.int32))

    sizes = jnp.where(number % 4 == 0, named(heavy_load, number // 4), named(usual, number - number // 4 - 1))
    mixed = jax.random.permutation(jax.random.fold_in(own, 3), count)
    donor, taker = mixed[0:count // 2 * 2:2], mixed[1:count // 2 * 2:2]
    margin = jnp.minimum(sizes[donor] - 1, bound - sizes[taker]) // 2
    margin = jnp.where((donor == sequence[0]) | (taker == sequence[0]) | (sizes[taker] == 0), 0, jnp.maximum(margin, 0))
    moved = jax.random.randint(jax.random.fold_in(own, 4), (count // 2,), 0, 1 << 20) % (margin + 1)
    sizes = sizes.at[donor].add(-moved).at[taker].add(moved)
    members = jnp.searchsorted(jnp.cumsum(sizes), jnp.arange(rows * top), side="right").astype(jnp.int32)
    grid = members.reshape(top, rows).T
    grid = grid[jax.random.permutation(jax.random.fold_in(own, 1), rows)]
    rotation = jax.random.randint(jax.random.fold_in(own, 2), (rows, 1), 0, top)
    return jnp.take_along_axis(grid, (jnp.arange(top)[None, :] + rotation) % top, axis=1)


def shares(amount, total, reach, skew, full):
    portions = [(1 << 20) // math.isqrt(grade ** skew) + 1 for grade in range(1, amount + 1)]
    largest = reach if full else min(reach, max(-(-total // amount), total * portions[0] // sum(portions)))
    least = 1 if total - largest >= amount - 1 else 0
    given, surplus = [largest] + [least] * (amount - 1), total - largest - least * (amount - 1)
    while surplus > 0:
        movable = [i for i in range(1, amount) if given[i] < largest] or [i for i in range(1, amount) if given[i] < reach]
        mass, remaining = sum([portions[i] for i in movable]), surplus
        for i in movable:
            addition = min(reach - given[i], max(1, remaining * portions[i] // mass), surplus)
            given[i] = given[i] + addition
            surplus = surplus - addition
    return np.array(given)


def noise(own_key, dims, width, reach, split=(), held_as=jnp.bfloat16):
    array = width * jax.random.normal(own_key, dims, jnp.float32)
    if split:
        array = array * levels(own_key, dims, split, -0.22, 0.18)
    return jnp.clip(array, -reach, reach).astype(held_as)


def setup_inputs(seed: int = 0) -> dict:
    seeds = jax.random.split(jax.random.key(seed), 22)
    tokens = noise(seeds[0], (TOKENS, D), 1.0, 6.0, ((0, 32),))
    doc_ids = jnp.searchsorted(jnp.cumsum(uneven(seeds[1], DOCS, TOKENS, TOKENS // 2, 1)), jnp.arange(TOKENS), side="right").astype(jnp.int32)
    mix_gain = jnp.clip(1.0 + 0.15 * jax.random.normal(seeds[2], (D,), jnp.float32), 0.25, 1.75).astype(jnp.bfloat16)
    zgate_proj = noise(seeds[3], (D, DI), D ** -0.5, 0.15625, ((1, 4),))
    xin_proj = noise(seeds[4], (D, DI), D ** -0.5, 0.15625, ((1, 4),))
    bc_proj = noise(seeds[5], (D, 2 * NSTATE), D ** -0.5, 0.15625)
    dt_proj = noise(seeds[6], (D, HEADS), D ** -0.5, 0.15625, ((1, 4),))
    conv_x = noise(seeds[7], (KCONV, DI), KCONV ** -0.5, 3.0, ((1, 4),))
    conv_bc = noise(seeds[8], (KCONV, 2 * NSTATE), KCONV ** -0.5, 3.0)
    dt_bias = jnp.clip(-3.0 + 2.0 * jax.random.uniform(seeds[9], (HEADS,), jnp.float32) ** levels(seeds[9], (HEADS,), ((0, 4),), -0.2, 0.2), -3.0, -1.0)
    decay_rate = jnp.clip(jnp.exp(math.log(0.5) - 8.517193 * jax.random.uniform(seeds[10], (HEADS,), jnp.float32) ** levels(seeds[10], (HEADS,), ((0, 4),), -0.2, 0.2)), 0.0001, 0.5)
    skip_gain = jnp.clip(jnp.exp(math.log(16.0) - 2.7725887 * jax.random.uniform(seeds[11], (HEADS,), jnp.float32) ** levels(seeds[11], (HEADS,), ((0, 4),), -0.2, 0.2)), 1.0, 16.0)
    norm_gain = jnp.clip(1.0 + 0.15 * jax.random.normal(seeds[12], (DI,), jnp.float32), 0.25, 1.75).astype(jnp.bfloat16)
    out_proj = noise(seeds[13], (DI, D), DI ** -0.5, 0.109375, ((0, 4),))
    moe_gain = jnp.clip(1.0 + 0.15 * jax.random.normal(seeds[14], (D,), jnp.float32), 0.25, 1.75).astype(jnp.bfloat16)
    router = noise(seeds[15], (D, EXPERTS), D ** -0.5, 0.15625)
    routes_keys = jax.random.split(jax.random.fold_in(seeds[16], 1), TOKENS // TOK_DEV)
    routes_turns = jax.random.permutation(jax.random.fold_in(seeds[16], 3), TOKENS // TOK_DEV)
    routes = jax.vmap(lambda own, number: routed_block(jax.random.fold_in(seeds[16], 2), own, number, TOK_DEV, EXPERTS, TOP, CAP, 2))(routes_keys, routes_turns).reshape((TOKENS, TOP))
    expert_gate_up = noise(seeds[17], (EXPERTS, 2, D, FFE), D ** -0.5, 0.15625, ((0, 32), (3, 4)))
    expert_down = noise(seeds[18], (EXPERTS, FFE, D), FFE ** -0.5, 0.25, ((0, 32), (1, 4)))
    shared_gate_up = noise(seeds[19], (2, D, FFS), D ** -0.5, 0.15625, ((2, 4),))
    shared_down = noise(seeds[20], (FFS, D), FFS ** -0.5, 0.1875, ((0, 4),))
    return {"tokens": tokens, "doc_ids": doc_ids, "mix_gain": mix_gain, "zgate_proj": zgate_proj, "xin_proj": xin_proj, "bc_proj": bc_proj, "dt_proj": dt_proj, "conv_x": conv_x, "conv_bc": conv_bc, "dt_bias": dt_bias, "decay_rate": decay_rate, "skip_gain": skip_gain, "norm_gain": norm_gain, "out_proj": out_proj, "moe_gain": moe_gain, "router": router, "routes": routes, "expert_gate_up": expert_gate_up, "expert_down": expert_down, "shared_gate_up": shared_gate_up, "shared_down": shared_down}


epsilon = 1e-05
highest = lax.Precision.HIGHEST

def rms_apply(values, gain):
    mean_square = lax.optimization_barrier(jnp.mean(values * values, axis=-1, keepdims=True))
    return values * lax.rsqrt(mean_square + epsilon) * gain.astype(jnp.float32)

def causal_conv(ext_vals, conv_weight, ext_ids):
    taps_count = conv_weight.shape[0]
    length = ext_vals.shape[0] - taps_count + 1
    own_ids = ext_ids[taps_count - 1:]
    summed = jnp.zeros((length, ext_vals.shape[1]), jnp.float32)
    for offset in range(taps_count):
        window_rows = ext_vals[offset:offset + length].astype(jnp.float32)
        in_doc = (ext_ids[offset:offset + length] == own_ids)[:, None]
        summed = summed + jnp.where(in_doc, window_rows, 0.0) * conv_weight[offset].astype(jnp.float32)
    return jax.nn.silu(summed).astype(jnp.bfloat16)

def ssd_run(head_x, b_in, c_out, log_decay, step_size, doc_ids, state, last_doc, block):
    length, heads_here, channels = head_x.shape
    count = length // block

    def one_block(carry, pieces):
        state_now, prev_doc = carry
        x_blk, b_blk, c_blk, decay_blk, step_blk, ids_blk = pieces
        cumul = jnp.cumsum(decay_blk, axis=0)
        causal = jnp.arange(block)[:, None] >= jnp.arange(block)[None, :]
        in_doc = (ids_blk[:, None] == ids_blk[None, :]) & causal
        spread = jnp.where(in_doc[:, :, None], cumul[:, None, :] - cumul[None, :, :], -1e+30)
        scores = jnp.dot(c_blk, b_blk.T, precision=highest)
        mixing = scores[:, :, None] * jnp.exp(spread) * step_blk[None, :, :]
        inner = jnp.einsum('tsh,shp->thp', mixing, x_blk, precision=highest)
        carried = (ids_blk == prev_doc).astype(jnp.float32)[:, None] * jnp.exp(cumul)
        outer = jnp.einsum('tn,hpn->thp', c_blk, state_now, precision=highest) * carried[:, :, None]
        to_end = jnp.where((ids_blk == ids_blk[-1])[:, None], cumul[-1][None, :] - cumul, -1e+30)
        end_weight = jnp.exp(to_end) * step_blk
        fresh = jnp.einsum('sh,shp,sn->hpn', end_weight, x_blk, b_blk, precision=highest)
        keep = jnp.exp(cumul[-1]) * (ids_blk[-1] == prev_doc).astype(jnp.float32)
        state_new = state_now * keep[:, None, None] + fresh
        return ((state_new, ids_blk[-1]), inner + outer)
    pieces = (head_x.reshape(count, block, heads_here, channels), b_in.reshape(count, block, -1), c_out.reshape(count, block, -1), log_decay.reshape(count, block, heads_here), step_size.reshape(count, block, heads_here), doc_ids.reshape(count, block))
    (state_end, doc_end), outputs = lax.scan(one_block, (state, last_doc), pieces)
    return (outputs.reshape(length, heads_here, channels), state_end, doc_end)

def reference(tokens, doc_ids, mix_gain, zgate_proj, xin_proj, bc_proj, dt_proj, conv_x, conv_bc, dt_bias, decay_rate, skip_gain, norm_gain, out_proj, moe_gain, router, routes, expert_gate_up, expert_down, shared_gate_up, shared_down):
    doc_ids = doc_ids.astype(jnp.int32)
    resid_in = tokens.astype(jnp.float32)
    normed_in = rms_apply(resid_in, mix_gain).astype(jnp.bfloat16)
    zgate = jnp.dot(normed_in, zgate_proj, preferred_element_type=jnp.float32).astype(jnp.bfloat16)
    x_pre = jnp.dot(normed_in, xin_proj, preferred_element_type=jnp.float32).astype(jnp.bfloat16)
    bc_pre = jnp.dot(normed_in, bc_proj, preferred_element_type=jnp.float32).astype(jnp.bfloat16)
    dt_raw = jnp.dot(normed_in, dt_proj, preferred_element_type=jnp.float32)
    pad_ids = jnp.concatenate([jnp.full((KCONV - 1,), -1, jnp.int32), doc_ids])
    x_conv = causal_conv(jnp.concatenate([jnp.zeros((KCONV - 1, DI), jnp.bfloat16), x_pre]), conv_x, pad_ids)
    bc_conv = causal_conv(jnp.concatenate([jnp.zeros((KCONV - 1, 2 * NSTATE), jnp.bfloat16), bc_pre]), conv_bc, pad_ids)
    step_size = jax.nn.softplus(dt_raw + dt_bias)
    log_decay = -decay_rate * step_size
    head_x = x_conv.astype(jnp.float32).reshape(TOKENS, HEADS, HEAD)
    b_in = bc_conv[:, :NSTATE].astype(jnp.float32)
    c_out = bc_conv[:, NSTATE:].astype(jnp.float32)
    start_state = jnp.zeros((HEADS, HEAD, NSTATE), jnp.float32)
    scanned, _, _ = ssd_run(head_x, b_in, c_out, log_decay, step_size, doc_ids, start_state, jnp.int32(-1), 64)
    scanned = scanned + skip_gain[None, :, None] * head_x
    gated = scanned.reshape(TOKENS, DI) * jax.nn.silu(zgate.astype(jnp.float32))
    normed_mid = rms_apply(gated, norm_gain).astype(jnp.bfloat16)
    resid = resid_in + jnp.dot(normed_mid, out_proj, preferred_element_type=jnp.float32)
    moe_in = rms_apply(resid, moe_gain).astype(jnp.bfloat16)
    logits = jnp.dot(moe_in, router, preferred_element_type=jnp.float32)
    chosen = jnp.take_along_axis(logits, routes.astype(jnp.int32), axis=1)
    sigmas = jax.nn.sigmoid(chosen)
    route_wts = sigmas / lax.optimization_barrier(jnp.sum(sigmas, axis=1, keepdims=True))
    shared_gate = jnp.dot(moe_in, shared_gate_up[0], preferred_element_type=jnp.float32)
    shared_up = jnp.dot(moe_in, shared_gate_up[1], preferred_element_type=jnp.float32)
    shared_act = (jax.nn.silu(shared_gate) * shared_up).astype(jnp.bfloat16)
    shared_out = jnp.dot(shared_act, shared_down, preferred_element_type=jnp.float32)
    flat_routes = routes.reshape(-1).astype(jnp.int32)
    one_hot = (flat_routes[:, None] == jnp.arange(EXPERTS, dtype=jnp.int32)[None, :]).astype(jnp.int32)
    earlier = jnp.cumsum(one_hot, axis=0).astype(jnp.int32) - one_hot
    slot = lax.optimization_barrier(jnp.sum(earlier * one_hot, axis=1)).astype(jnp.int32)
    capacity = N_SEQ * CAP
    dest = flat_routes * capacity + slot
    token_of = (jnp.arange(TOKENS * TOP, dtype=jnp.int32) // TOP).astype(jnp.int32)
    source = jnp.full((EXPERTS * capacity,), -1, jnp.int32).at[dest].set(token_of).reshape(EXPERTS, capacity)
    slot_wts = jnp.zeros((EXPERTS * capacity,), jnp.float32).at[dest].set(route_wts.reshape(-1))
    slot_wts = slot_wts.reshape(EXPERTS, capacity)

    def one_expert(accum, pieces):
        src_rows, wts_rows, gate_up, down = pieces
        valid = src_rows >= 0
        safe_rows = jnp.where(valid, src_rows, 0).astype(jnp.int32)
        chosen_rows = jnp.where(valid[:, None], moe_in[safe_rows], jnp.zeros((), jnp.bfloat16))
        gate_part = jnp.dot(chosen_rows, gate_up[0], preferred_element_type=jnp.float32)
        up_part = jnp.dot(chosen_rows, gate_up[1], preferred_element_type=jnp.float32)
        act = (jax.nn.silu(gate_part) * up_part).astype(jnp.bfloat16)
        act_groups = act.astype(jnp.float32).reshape(capacity, N_TP, FFQ)
        down_groups = down.astype(jnp.float32).reshape(N_TP, FFQ, D)
        grouped = jnp.einsum('rgf,gfd->rgd', act_groups, down_groups, precision=highest)
        grouped = lax.optimization_barrier(grouped.astype(jnp.bfloat16)).astype(jnp.float32)
        expert_out = lax.optimization_barrier(jnp.sum(grouped, axis=1))
        weights_here = jnp.where(valid, wts_rows, 0.0)
        accum = accum.at[safe_rows].add(expert_out * weights_here[:, None])
        return (accum, None)
    moe_sum, _ = lax.scan(one_expert, jnp.zeros((TOKENS, D), jnp.float32), (source, slot_wts, expert_gate_up, expert_down))
    return (resid + moe_sum + shared_out).astype(jnp.bfloat16)
```

```python
import functools

import jax
import jax.numpy as jnp
from jax import lax
from jax.experimental import pallas as pl
from jax.experimental.pallas import tpu as pltpu
from jax.sharding import PartitionSpec as P

D = 1536
HEAD = 64
NSTATE = 128
DI = 3072
epsilon = 1e-05
highest = lax.Precision.HIGHEST
F32 = jnp.float32
BF = jnp.bfloat16


def rms_apply(values, gain):
    mean_square = jnp.mean(values * values, axis=-1, keepdims=True)
    return values * lax.rsqrt(mean_square + epsilon) * gain.astype(F32)


def silu(v):
    return v / (1.0 + jnp.exp(-v))


def mixer_kernel(
    heads, xe_ref, be_ref, ids_ref, idrow_ref, dt_ref, rate_ref, cx_ref, cb_ref, skip_ref,
    y_ref, st_ref, c_ref, car_ref, tot_ref, xs_ref, bs_ref,
):
    n = y_ref.shape[0]
    width = y_ref.shape[1]
    xs_ref[...] = xe_ref[...].astype(F32)
    bs_ref[...] = be_ref[...].astype(F32)
    own = ids_ref[pl.ds(8, n), :]
    xsum = jnp.zeros((n, width), F32)
    bsum = jnp.zeros((n, 2 * NSTATE), F32)
    for k in range(4):
        live = ids_ref[pl.ds(5 + k, n), :] == own
        xsum += jnp.where(live, xs_ref[pl.ds(5 + k, n), :], 0.0) * cx_ref[k : k + 1, :]
        bsum += jnp.where(live, bs_ref[pl.ds(5 + k, n), :], 0.0) * cb_ref[k : k + 1, :]
    x_conv = silu(xsum).astype(BF).astype(F32)
    bc = silu(bsum).astype(BF)
    b_in, c_out = bc[:, :NSTATE], bc[:, NSTATE:]
    c_ref[...] = c_out
    raw = dt_ref[...]
    step = jnp.maximum(raw, 0.0) + jnp.log1p(jnp.exp(-jnp.abs(raw)))
    decay = -rate_ref[...] * step
    row = lax.broadcasted_iota(jnp.int32, (n, n), 0)
    col = lax.broadcasted_iota(jnp.int32, (n, n), 1)
    causal = row >= col
    tri = jnp.where(causal, 1.0, 0.0)
    cum = jnp.dot(tri, decay, precision=highest, preferred_element_type=F32)
    cum_t = cum.T
    last = cum[n - 1 : n, :]
    tot_ref[...] = last
    expand = jnp.where(
        lax.broadcasted_iota(jnp.int32, (128, width), 1) // HEAD
        == lax.broadcasted_iota(jnp.int32, (128, width), 0),
        1.0,
        0.0,
    )
    step_w = jnp.dot(step, expand, precision=highest, preferred_element_type=F32)
    at_end = own == ids_ref[n + 7 : n + 8, :]
    to_end = jnp.where(at_end, jnp.exp(last - cum), 0.0)
    end_w = jnp.dot(to_end, expand, precision=highest, preferred_element_type=F32)
    car_ref[...] = jnp.dot(jnp.exp(cum), expand, precision=highest, preferred_element_type=F32)
    x_step = x_conv * step_w
    x_in = x_step.astype(BF)
    st_ref[...] = lax.dot_general(
        b_in, (x_step * end_w).astype(BF), (((0,), (0,)), ((), ())), preferred_element_type=F32
    )
    scores = lax.dot_general(c_out, b_in, (((1,), (1,)), ((), ())), preferred_element_type=F32)
    scores = jnp.where(causal & (own == idrow_ref[...]), scores, 0.0)
    skip = x_conv * skip_ref[...]
    half = n // 2
    for top, bottom in ((0, half), (half, n)):
        for pair in range(heads // 2):
            parts = []
            for h in (2 * pair, 2 * pair + 1):
                diff = cum[top:bottom, h : h + 1] - cum_t[h : h + 1, :bottom]
                mixing = (scores[top:bottom, :bottom] * jnp.exp(jnp.minimum(diff, 0.0))).astype(BF)
                parts.append(
                    jnp.dot(
                        mixing, x_in[:bottom, h * HEAD : (h + 1) * HEAD], preferred_element_type=F32
                    )
                )
            cols = slice(pair * 128, pair * 128 + 128)
            y_ref[top:bottom, cols] = jnp.concatenate(parts, axis=1) + skip[top:bottom, cols]


def mixer_local(x_ext, bc_ext, ids_ext, ids_row, dt, rate, conv_x, conv_bc, skip, heads):
    n, width = x_ext.shape[0] - 8, x_ext.shape[1]
    vm = pl.BlockSpec(memory_space=pltpu.VMEM)
    return pl.pallas_call(
        functools.partial(mixer_kernel, heads),
        out_shape=(
            jax.ShapeDtypeStruct((n, width), F32),
            jax.ShapeDtypeStruct((NSTATE, width), F32),
            jax.ShapeDtypeStruct((n, NSTATE), BF),
            jax.ShapeDtypeStruct((n, width), F32),
            jax.ShapeDtypeStruct((1, 128), F32),
        ),
        in_specs=[vm] * 9,
        out_specs=(vm,) * 5,
        scratch_shapes=[pltpu.VMEM((n + 8, width), F32), pltpu.VMEM((n + 8, 2 * NSTATE), F32)],
        name="mixer_local",
    )(x_ext, bc_ext, ids_ext, ids_row, dt, rate, conv_x, conv_bc, skip)


def expert_kernel(x_ref, w_ref, gu_hbm, dn_hbm, o_ref, gu, dn, sem):
    parts, experts = gu_hbm.shape[0], gu_hbm.shape[1]
    wide = gu_hbm.shape[4]

    def copies():
        out = []
        for t in range(parts):
            for e in range(experts):
                for c in range(2):
                    out.append(
                        pltpu.make_async_copy(
                            gu_hbm.at[t, e, c],
                            gu.at[e, :, pl.ds((c * parts + t) * wide, wide)],
                            sem.at[len(out)],
                        )
                    )
                out.append(
                    pltpu.make_async_copy(
                        dn_hbm.at[t, e], dn.at[e, pl.ds(t * wide, wide), :], sem.at[len(out)]
                    )
                )
        return out

    @pl.when(pl.program_id(0) == 0)
    def _():
        for copy in copies():
            copy.start()
        for copy in copies():
            copy.wait()

    x = x_ref[...]
    total = None
    hidden = parts * wide
    for e in range(experts):
        both = jnp.dot(x, gu[e], preferred_element_type=F32)
        act = (silu(both[:, :hidden]) * both[:, hidden:] * w_ref[:, e : e + 1]).astype(BF)
        out = jnp.dot(act, dn[e], preferred_element_type=F32)
        total = out if total is None else total + out
    o_ref[...] = total.astype(BF)


def experts_dense(x, wts, gate_up, down):
    rows = x.shape[0]
    parts, experts, _, _, wide = gate_up.shape
    tile = 256
    hidden = parts * wide
    return pl.pallas_call(
        expert_kernel,
        out_shape=jax.ShapeDtypeStruct((rows, D), BF),
        grid=(rows // tile,),
        in_specs=[
            pl.BlockSpec((tile, D), lambda i: (i, 0)),
            pl.BlockSpec((tile, experts), lambda i: (i, 0)),
            pl.BlockSpec(memory_space=pl.ANY),
            pl.BlockSpec(memory_space=pl.ANY),
        ],
        out_specs=pl.BlockSpec((tile, D), lambda i: (i, 0)),
        scratch_shapes=[
            pltpu.VMEM((experts, D, 2 * hidden), BF),
            pltpu.VMEM((experts, hidden, D), BF),
            pltpu.SemaphoreType.DMA((parts * experts * 3,)),
        ],
        compiler_params=pltpu.CompilerParams(vmem_limit_bytes=40 << 20),
        name="experts_dense",
    )(x, wts, gate_up, down)


def body(
    tokens, doc_ids, mix_gain, zgate_proj, xin_proj, bc_proj, dt_proj, conv_x, conv_bc, dt_bias,
    decay_rate, skip_gain, norm_gain, out_proj, moe_gain, router, routes, expert_gate_up,
    expert_down, shared_gate_up, shared_down,
):
    rows = tokens.shape[0]
    tp_index, seq_index = lax.axis_index("tp"), lax.axis_index("seq")
    tp_count, seq_count = lax.axis_size("tp"), lax.axis_size("seq")
    heads = dt_proj.shape[1]
    width = heads * HEAD
    part = rows // tp_count
    experts_local = expert_down.shape[0]

    gate_up_all = lax.all_gather(expert_gate_up, "tp")
    down_all = lax.all_gather(expert_down, "tp")
    own_routes = lax.dynamic_slice_in_dim(routes, tp_index * part, part, 0)
    plane_routes = lax.all_gather(own_routes, "seq", tiled=True)

    resid_in = tokens.astype(F32)
    normed_in = rms_apply(resid_in, mix_gain).astype(BF)
    zgate = jnp.dot(normed_in, zgate_proj, preferred_element_type=F32).astype(BF)
    x_pre = jnp.dot(normed_in, xin_proj, preferred_element_type=F32).astype(BF)
    bc_pre = jnp.dot(normed_in, bc_proj, preferred_element_type=F32).astype(BF)
    dt_raw = jnp.dot(normed_in, dt_proj, preferred_element_type=F32) + dt_bias
    dt_raw = jnp.pad(dt_raw, ((0, 0), (0, 128 - heads)))
    rate = jnp.pad(decay_rate, (0, 128 - heads))[None, :]
    marks = jnp.broadcast_to((doc_ids[-8:, None] + 1).astype(BF), (8, 128))
    tail = jnp.concatenate([x_pre[-8:], bc_pre[-8:], marks], axis=1)
    prev = lax.ppermute(tail, "seq", [(s, s + 1) for s in range(seq_count - 1)])
    prev_ids = prev[:, width + 256].astype(jnp.int32) - 1
    ids_ext = jnp.concatenate([prev_ids, doc_ids])
    x_ext = jnp.concatenate([prev[:, :width], x_pre])
    bc_ext = jnp.concatenate([prev[:, width : width + 256], bc_pre])
    local_y, state, c_out, carry_w, total = mixer_local(
        x_ext, bc_ext, ids_ext[:, None], doc_ids[None, :], dt_raw, rate,
        conv_x.astype(F32), conv_bc.astype(F32), jnp.repeat(skip_gain, HEAD)[None, :], heads,
    )

    note = jnp.concatenate([total[0, :heads], doc_ids[-1:].astype(F32)])
    notes = lax.all_gather(note, "seq")
    ends = notes[:, heads]
    gone = jnp.cumsum(notes[:, :heads], axis=0)
    ends_before = jnp.concatenate([jnp.full((1,), -1.0, F32), ends[:-1]])
    gone_before = jnp.concatenate([jnp.zeros((1, heads), F32), gone[:-1]])
    index = jnp.arange(seq_count)
    reach = (index[None, :] < index[:, None]) & (ends[None, :] == ends_before[:, None])
    link = jnp.where(
        reach[:, :, None],
        jnp.exp(jnp.minimum(gone_before[:, None, :] - gone[None, :, :], 0.0)),
        0.0,
    )
    share = state.reshape(seq_count, NSTATE // seq_count, width)
    share = lax.all_to_all(share, "seq", split_axis=0, concat_axis=0, tiled=True)
    share = share.reshape(seq_count, NSTATE // seq_count, heads, HEAD)
    share = jnp.einsum("qsh,snhp->qnhp", link, share, precision=highest)
    share = share.reshape(seq_count, NSTATE // seq_count, width)
    incoming = lax.all_to_all(share, "seq", split_axis=0, concat_axis=0, tiled=True)
    incoming = incoming.reshape(NSTATE, width)
    before = jnp.dot(c_out, incoming.astype(BF), preferred_element_type=F32)
    carried = doc_ids.astype(F32) == ends_before[seq_index]
    scanned = local_y + jnp.where(carried[:, None], before * carry_w, 0.0)
    gated = scanned * jax.nn.silu(zgate.astype(F32))
    squares = jnp.sum(gated * gated, axis=1)
    inner = (gated * norm_gain.astype(F32)).astype(BF)
    projected = jnp.dot(inner, out_proj, preferred_element_type=F32)
    squares = lax.psum_scatter(squares, "tp", tiled=True)
    projected = lax.psum_scatter(projected, "tp", scatter_dimension=0, tiled=True)
    own_rows = lax.dynamic_slice_in_dim(resid_in, tp_index * part, part, 0)
    resid = own_rows + projected * lax.rsqrt(squares[:, None] / DI + epsilon)
    moe_in = rms_apply(resid, moe_gain).astype(BF)

    plane = lax.all_gather(moe_in, "seq", tiled=True)
    line = lax.all_gather(moe_in, "tp", tiled=True)
    logits = jnp.dot(plane, router, preferred_element_type=F32)
    iota = jnp.arange(router.shape[1], dtype=jnp.int32)
    named = jnp.any(plane_routes[:, :, None] == iota[None, None, :], axis=1)
    sigmas = jnp.where(named, jax.nn.sigmoid(logits), 0.0)
    wts = sigmas / jnp.sum(sigmas, axis=1, keepdims=True)
    wts = lax.dynamic_slice_in_dim(wts, seq_index * experts_local, experts_local, 1)
    routed = experts_dense(plane, wts, gate_up_all, down_all)
    routed = lax.psum_scatter(routed, "seq", scatter_dimension=0, tiled=True)
    shared_gate = jnp.dot(line, shared_gate_up[0], preferred_element_type=F32)
    shared_up = jnp.dot(line, shared_gate_up[1], preferred_element_type=F32)
    shared_act = (jax.nn.silu(shared_gate) * shared_up).astype(BF)
    shared_part = jnp.dot(shared_act, shared_down, preferred_element_type=F32)
    mine = lax.dynamic_slice_in_dim(shared_part, tp_index * part, part, 0)
    whole = lax.dynamic_update_slice_in_dim(
        shared_part, mine + resid + routed.astype(F32), tp_index * part, 0
    )
    added = lax.psum_scatter(whole, "tp", scatter_dimension=1, tiled=True)
    return added.astype(BF)


def solution(mesh):
    in_specs = (
        P("seq", None), P("seq"), P(), P(None, "tp"), P(None, "tp"), P(), P(None, "tp"),
        P(None, "tp"), P(), P("tp"), P("tp"), P("tp"), P("tp"), P("tp", None), P(), P(),
        P("seq", None), P("seq", None, None, "tp"), P("seq", "tp", None), P(None, None, "tp"),
        P("tp", None),
    )
    return jax.shard_map(
        body, mesh=mesh, in_specs=in_specs, out_specs=P("seq", "tp"), check_vma=False
    )
```

```python
import functools

import jax
import jax.numpy as jnp
from jax import lax
from jax.experimental import pallas as pl
from jax.experimental.pallas import tpu as pltpu
from jax.sharding import PartitionSpec as P

D = 1536
HEAD = 64
NSTATE = 128
DI = 3072
epsilon = 1e-05
highest = lax.Precision.HIGHEST
F32 = jnp.float32
BF = jnp.bfloat16


def rms_apply(values, gain):
    mean_square = jnp.mean(values * values, axis=-1, keepdims=True)
    return values * lax.rsqrt(mean_square + epsilon) * gain.astype(F32)


def silu(v):
    return v / (1.0 + jnp.exp(-v))


MESH = pl.DeviceIdType.MESH


def mixer_kernel(
    heads, seqs, tps, x_ref, bc_ref, idc_ref, idr_ref, dt_ref, rate_ref, cx_ref, cb_ref, skip_ref,
    z_ref, gain_ref, out_ref, tok_ref, moe_gain_ref, resid_ref, moe_ref,
    xs, bs, ids, tail, head_rows, ysum, slabs, got, back, entry, proj, sent, landed, sq_out, sq_in,
    tail_sems, go_sems, come_sems, ret_go, ret_come, tp_go, tp_come, sq_go, sq_come,
):
    me, mt = lax.axis_index("seq"), lax.axis_index("tp")
    n, width = x_ref.shape
    part = n // tps
    half_w = width // 2
    barrier = pltpu.get_barrier_semaphore()

    def greet(d, c):
        pl.semaphore_signal(
            barrier, inc=1, device_id={"seq": lax.rem(me + d, seqs)}, device_id_type=MESH
        )
        return c

    lax.fori_loop(1, seqs, greet, 0)
    for d in range(1, tps):
        pl.semaphore_signal(
            barrier, inc=1, device_id={"tp": lax.rem(mt + d, tps)}, device_id_type=MESH
        )
    xs[pl.ds(8, n), :] = x_ref[...].astype(F32)
    bs[pl.ds(8, n), :] = bc_ref[...].astype(F32)
    own = idc_ref[...]
    ids[pl.ds(8, n), :] = jnp.broadcast_to(own, (n, 128))
    tail[:, 0:width] = xs[pl.ds(n, 8), :]
    tail[:, width : width + 2 * NSTATE] = bs[pl.ds(n, 8), :]
    tail[:, width + 2 * NSTATE :] = ids[pl.ds(n, 8), :]
    pl.semaphore_wait(barrier, seqs - 1 + tps - 1)
    halo = pltpu.make_async_remote_copy(
        src_ref=tail, dst_ref=head_rows, send_sem=tail_sems.at[0], recv_sem=tail_sems.at[1],
        device_id={"seq": lax.rem(me + 1, seqs)}, device_id_type=MESH,
    )
    halo.start()

    raw = dt_ref[...]
    step = jnp.maximum(raw, 0.0) + jnp.log1p(jnp.exp(-jnp.abs(raw)))
    decay = -rate_ref[...] * step
    row = lax.broadcasted_iota(jnp.int32, (n, n), 0)
    col = lax.broadcasted_iota(jnp.int32, (n, n), 1)
    causal = row >= col
    tri = jnp.where(causal, 1.0, 0.0)
    cum = jnp.dot(tri, decay, precision=highest, preferred_element_type=F32)
    cum_t = cum.T
    last = cum[n - 1 : n, :]
    expand = jnp.where(
        lax.broadcasted_iota(jnp.int32, (128, width), 1) // HEAD
        == lax.broadcasted_iota(jnp.int32, (128, width), 0),
        1.0,
        0.0,
    )
    step_w = jnp.dot(step, expand, precision=highest, preferred_element_type=F32)
    at_end = own == idc_ref[n - 1 : n, :]
    to_end = jnp.where(at_end, jnp.exp(last - cum), 0.0)
    end_w = jnp.dot(to_end, expand, precision=highest, preferred_element_type=F32)
    carry_w = jnp.dot(jnp.exp(cum), expand, precision=highest, preferred_element_type=F32)
    r8 = lax.broadcasted_iota(jnp.int32, (NSTATE, 2 * NSTATE), 1)
    n8 = lax.broadcasted_iota(jnp.int32, (NSTATE, 2 * NSTATE), 0)
    same = n8 == 4 * (r8 // 8) + r8 % 4
    dup_l = jnp.where(same & (r8 % 8 < 4), 1.0, 0.0).astype(BF)
    dup_r = jnp.where(same & (r8 % 8 >= 4), 1.0, 0.0).astype(BF)
    dup = dup_l + dup_r
    low = lax.broadcasted_iota(jnp.int32, (2 * NSTATE, half_w), 0) % 8 < 4

    halo.wait()
    xs[pl.ds(0, 8), :] = head_rows[:, 0:width]
    bs[pl.ds(0, 8), :] = head_rows[:, width : width + 2 * NSTATE]
    ids[pl.ds(0, 8), :] = jnp.where(me == 0, -1.0, head_rows[:, width + 2 * NSTATE :])
    before_id = ids[pl.ds(7, 1), :]
    xsum = jnp.zeros((n, width), F32)
    bsum = jnp.zeros((n, 2 * NSTATE), F32)
    for k in range(4):
        live = ids[pl.ds(5 + k, n), 0:1] == own
        xsum += jnp.where(live, xs[pl.ds(5 + k, n), :], 0.0) * cx_ref[k : k + 1, :]
        bsum += jnp.where(live, bs[pl.ds(5 + k, n), :], 0.0) * cb_ref[k : k + 1, :]
    x_conv = silu(xsum).astype(BF).astype(F32)
    bc = silu(bsum).astype(BF)
    b_in, c_out = bc[:, :NSTATE], bc[:, NSTATE:]
    x_step = x_conv * step_w
    x_in = x_step.astype(BF)
    b_dup = jnp.dot(b_in, dup, preferred_element_type=F32).astype(BF)
    state = lax.dot_general(
        b_dup, (x_step * end_w).astype(BF), (((0,), (0,)), ((), ())), preferred_element_type=F32
    )
    state = jnp.where(low, state[:, :half_w], state[:, half_w:])
    slabs[:, :, 0:half_w] = state.reshape(seqs, 8, half_w)
    lane = lax.broadcasted_iota(jnp.int32, (1, 128), 1)
    note = jnp.where(lane == 127, idc_ref[n - 1 : n, :], last)
    slabs[:, :, half_w:] = jnp.broadcast_to(note[None], (seqs, 8, 128))

    def outward(d):
        peer = lax.rem(me + d, seqs)
        return pltpu.make_async_remote_copy(
            src_ref=slabs.at[peer], dst_ref=got.at[me], send_sem=go_sems.at[d],
            recv_sem=come_sems.at[d], device_id={"seq": peer}, device_id_type=MESH,
        )

    def homeward(d):
        peer = lax.rem(me + d, seqs)
        return pltpu.make_async_remote_copy(
            src_ref=back.at[peer], dst_ref=entry.at[me], send_sem=ret_go.at[d],
            recv_sem=ret_come.at[d], device_id={"seq": peer}, device_id_type=MESH,
        )

    def each(make, act):
        def one(d, c):
            getattr(make(d), act)()
            return c

        lax.fori_loop(1, seqs, one, 0)

    each(outward, "start")
    got[me] = slabs[me]

    scores = lax.dot_general(c_out, b_in, (((1,), (1,)), ((), ())), preferred_element_type=F32)
    scores = jnp.where(causal & (own == idr_ref[...]), scores, 0.0)

    def inner(pairs):
        half = n // 2
        for top, bottom in ((0, half), (half, n)):
            for pair in pairs:
                parts = []
                for h in (2 * pair, 2 * pair + 1):
                    diff = cum[top:bottom, h : h + 1] - cum_t[h : h + 1, :bottom]
                    mixing = scores[top:bottom, :bottom] * jnp.exp(jnp.minimum(diff, 0.0))
                    parts.append(
                        jnp.dot(
                            mixing.astype(BF), x_in[:bottom, h * HEAD : (h + 1) * HEAD],
                            preferred_element_type=F32,
                        )
                    )
                cols = slice(pair * 128, pair * 128 + 128)
                ysum[top:bottom, cols] = (
                    jnp.concatenate(parts, axis=1)
                    + x_conv[top:bottom, cols] * skip_ref[:, cols]
                )

    inner(range(0, heads // 4))
    each(outward, "wait")
    notes = got[:, :, half_w:].reshape(8 * seqs, 128)
    faded = jnp.dot(
        jnp.where(lax.broadcasted_iota(jnp.int32, notes.shape, 1) < heads, notes, 0.0),
        expand, precision=highest, preferred_element_type=F32,
    )
    faded = jnp.exp(jnp.where(low, faded[:, :half_w], faded[:, half_w:])).reshape(seqs, 8, half_w)
    ends = jnp.broadcast_to(notes[:, 127:128], (8 * seqs, half_w)).reshape(seqs, 8, half_w)
    running = jnp.zeros((8, half_w), F32)
    for q in range(seqs):
        back[q] = running
        if q == 0:
            running = got[q, :, 0:half_w]
        else:
            keep = jnp.where(ends[q] == ends[q - 1], faded[q], 0.0)
            running = running * keep + got[q, :, 0:half_w]
    each(homeward, "start")
    entry[me] = back[me]
    inner(range(heads // 4, heads // 2))
    c_l = jnp.dot(c_out, dup_l, preferred_element_type=F32).astype(BF)
    c_r = jnp.dot(c_out, dup_r, preferred_element_type=F32).astype(BF)
    zg = z_ref[...].astype(F32)
    gate = silu(zg)
    follows = own == before_id[:, 0:1]
    each(homeward, "wait")
    inc = entry[...].reshape(8 * seqs, half_w).astype(BF)
    before = jnp.concatenate(
        [
            jnp.dot(c_l, inc, preferred_element_type=F32),
            jnp.dot(c_r, inc, preferred_element_type=F32),
        ],
        axis=1,
    )
    scanned = ysum[...] + jnp.where(follows, before * carry_w, 0.0)
    gated = scanned * gate
    squares = jnp.sum(gated * gated, axis=1, keepdims=True)
    sq_out[...] = jnp.broadcast_to(squares, (n, 128)).reshape(tps, part, 128)
    lhs = (gated * gain_ref[...]).astype(BF)
    chunk = 512
    for c in range(D // chunk):
        cols = slice(c * chunk, (c + 1) * chunk)
        piece = jnp.dot(lhs, out_ref[:, cols], preferred_element_type=F32)
        piece = piece.reshape(tps, part, chunk)
        proj[:, :, cols] = piece
        sent[:, :, cols] = piece.astype(BF)
    moves = []
    for d in (2, 1, 3):
        peer = lax.rem(mt + d, tps)
        for src, dst, go, come in (
            (sent, landed, tp_go, tp_come),
            (sq_out, sq_in, sq_go, sq_come),
        ):
            move = pltpu.make_async_remote_copy(
                src_ref=src.at[peer], dst_ref=dst.at[d - 1], send_sem=go.at[d - 1],
                recv_sem=come.at[d - 1], device_id={"tp": peer}, device_id_type=MESH,
            )
            move.start()
            moves.append(move)
    total = proj[mt]
    sq = sq_out[mt]
    for move in moves:
        move.wait()
    for d in range(tps - 1):
        total = total + landed[d].astype(F32)
        sq = sq + sq_in[d]
    resid = tok_ref[...].astype(F32) + total * lax.rsqrt(sq[:, 0:1] / DI + epsilon)
    resid_ref[...] = resid
    power = jnp.sum(resid * resid, axis=1, keepdims=True) / D
    moe_ref[...] = (resid * lax.rsqrt(power + epsilon) * moe_gain_ref[...]).astype(BF)


def mixer(seqs, tps, heads, *args):
    n, width = args[0].shape
    part = n // tps
    vm = pl.BlockSpec(memory_space=pltpu.VMEM)
    dma = pltpu.SemaphoreType.DMA
    return pl.pallas_call(
        functools.partial(mixer_kernel, heads, seqs, tps),
        out_shape=(jax.ShapeDtypeStruct((part, D), F32), jax.ShapeDtypeStruct((part, D), BF)),
        in_specs=[vm] * len(args),
        out_specs=(vm, vm),
        scratch_shapes=[
            pltpu.VMEM((n + 8, width), F32),
            pltpu.VMEM((n + 8, 2 * NSTATE), F32),
            pltpu.VMEM((n + 8, 128), F32),
            pltpu.VMEM((8, width + 2 * NSTATE + 128), F32),
            pltpu.VMEM((8, width + 2 * NSTATE + 128), F32),
            pltpu.VMEM((n, width), F32),
            pltpu.VMEM((seqs, 8, width // 2 + 128), F32),
            pltpu.VMEM((seqs, 8, width // 2 + 128), F32),
            pltpu.VMEM((seqs, 8, width // 2), F32),
            pltpu.VMEM((seqs, 8, width // 2), F32),
            pltpu.VMEM((tps, part, D), F32),
            pltpu.VMEM((tps, part, D), BF),
            pltpu.VMEM((tps - 1, part, D), BF),
            pltpu.VMEM((tps, part, 128), F32),
            pltpu.VMEM((tps - 1, part, 128), F32),
            dma((2,)),
            dma((seqs,)),
            dma((seqs,)),
            dma((seqs,)),
            dma((seqs,)),
            dma((tps - 1,)),
            dma((tps - 1,)),
            dma((tps - 1,)),
            dma((tps - 1,)),
        ],
        compiler_params=pltpu.CompilerParams(collective_id=0, has_side_effects=True),
        name="mixer",
    )(*args)


def expert_kernel(parts, x_ref, w_ref, *rest):
    gus, dns = rest[:parts], rest[parts : 2 * parts]
    o_ref, gu, dn, sem = rest[2 * parts :]
    experts, wide = gus[0].shape[0], gus[0].shape[3]

    def copies():
        out = []
        for t in range(parts):
            for e in range(experts):
                for c in range(2):
                    out.append(
                        pltpu.make_async_copy(
                            gus[t].at[e, c],
                            gu.at[e, :, pl.ds((c * parts + t) * wide, wide)],
                            sem.at[len(out)],
                        )
                    )
                out.append(
                    pltpu.make_async_copy(
                        dns[t].at[e], dn.at[e, pl.ds(t * wide, wide), :], sem.at[len(out)]
                    )
                )
        return out

    @pl.when(pl.program_id(0) == 0)
    def _():
        for copy in copies():
            copy.start()
        for copy in copies():
            copy.wait()

    x = x_ref[...]
    total = None
    hidden = parts * wide
    for e in range(experts):
        both = jnp.dot(x, gu[e], preferred_element_type=F32)
        act = (silu(both[:, :hidden]) * both[:, hidden:] * w_ref[:, e : e + 1]).astype(BF)
        out = jnp.dot(act, dn[e], preferred_element_type=F32)
        total = out if total is None else total + out
    o_ref[...] = total.astype(BF)


def experts_dense(x, wts, gate_up, down):
    rows = x.shape[0]
    parts = len(gate_up)
    experts, _, _, wide = gate_up[0].shape
    tile = 256
    hidden = parts * wide
    return pl.pallas_call(
        functools.partial(expert_kernel, parts),
        out_shape=jax.ShapeDtypeStruct((rows, D), BF),
        grid=(rows // tile,),
        in_specs=[
            pl.BlockSpec((tile, D), lambda i: (i, 0)),
            pl.BlockSpec((tile, experts), lambda i: (i, 0)),
        ]
        + [pl.BlockSpec(memory_space=pl.ANY)] * (2 * parts),
        out_specs=pl.BlockSpec((tile, D), lambda i: (i, 0)),
        scratch_shapes=[
            pltpu.VMEM((experts, D, 2 * hidden), BF),
            pltpu.VMEM((experts, hidden, D), BF),
            pltpu.SemaphoreType.DMA((parts * experts * 3,)),
        ],
        compiler_params=pltpu.CompilerParams(vmem_limit_bytes=40 << 20),
        name="experts_dense",
    )(x, wts, *gate_up, *down)


def body(
    tokens, doc_ids, mix_gain, zgate_proj, xin_proj, bc_proj, dt_proj, conv_x, conv_bc, dt_bias,
    decay_rate, skip_gain, norm_gain, out_proj, moe_gain, router, routes, expert_gate_up,
    expert_down, shared_gate_up, shared_down,
):
    rows = tokens.shape[0]
    tp_index, seq_index = lax.axis_index("tp"), lax.axis_index("seq")
    tp_count, seq_count = lax.axis_size("tp"), lax.axis_size("seq")
    heads = dt_proj.shape[1]
    width = heads * HEAD
    part = rows // tp_count
    experts_local = expert_down.shape[0]

    def shift(value, steps):
        pairs = [(t, (t + steps) % tp_count) for t in range(tp_count)]
        return lax.ppermute(value, "tp", pairs)

    gu_left, dn_left = shift(expert_gate_up, 1), shift(expert_down, 1)
    gu_right, dn_right = shift(expert_gate_up, -1), shift(expert_down, -1)
    own_routes = lax.dynamic_slice_in_dim(routes, tp_index * part, part, 0)
    plane_routes = lax.all_gather(own_routes, "seq", tiled=True)

    resid_in = tokens.astype(F32)
    normed_in = rms_apply(resid_in, mix_gain).astype(BF)
    zgate = jnp.dot(normed_in, zgate_proj, preferred_element_type=F32).astype(BF)
    x_pre = jnp.dot(normed_in, xin_proj, preferred_element_type=F32).astype(BF)
    bc_pre = jnp.dot(normed_in, bc_proj, preferred_element_type=F32).astype(BF)
    dt_raw = jnp.dot(normed_in, dt_proj, preferred_element_type=F32) + dt_bias
    dt_raw = jnp.pad(dt_raw, ((0, 0), (0, 128 - heads)))
    rate = jnp.pad(decay_rate, (0, 128 - heads))[None, :]
    own_rows = lax.dynamic_slice_in_dim(tokens, tp_index * part, part, 0)
    ids = doc_ids.astype(F32)
    resid, moe_in = mixer(
        seq_count, tp_count, heads, x_pre, bc_pre, ids[:, None], ids[None, :], dt_raw, rate,
        conv_x.astype(F32), conv_bc.astype(F32), jnp.repeat(skip_gain, HEAD)[None, :], zgate,
        norm_gain.astype(F32)[None, :], out_proj, own_rows, moe_gain.astype(F32)[None, :],
    )
    moe_in, resid, gu_left, dn_right = lax.optimization_barrier(
        (moe_in, resid, gu_left, dn_right)
    )
    gu_far, dn_far = shift(gu_left, 1), shift(dn_right, -1)

    plane = lax.all_gather(moe_in, "seq", tiled=True)
    line = lax.all_gather(moe_in, "tp", tiled=True)
    logits = jnp.dot(plane, router, preferred_element_type=F32)
    iota = jnp.arange(router.shape[1], dtype=jnp.int32)
    named = jnp.any(plane_routes[:, :, None] == iota[None, None, :], axis=1)
    sigmas = jnp.where(named, jax.nn.sigmoid(logits), 0.0)
    wts = sigmas / jnp.sum(sigmas, axis=1, keepdims=True)
    wts = lax.dynamic_slice_in_dim(wts, seq_index * experts_local, experts_local, 1)
    routed = experts_dense(
        plane, wts, (expert_gate_up, gu_left, gu_right, gu_far),
        (expert_down, dn_left, dn_right, dn_far),
    )
    routed = lax.psum_scatter(routed, "seq", scatter_dimension=0, tiled=True)
    shared_gate = jnp.dot(line, shared_gate_up[0], preferred_element_type=F32)
    shared_up = jnp.dot(line, shared_gate_up[1], preferred_element_type=F32)
    shared_act = (jax.nn.silu(shared_gate) * shared_up).astype(BF)
    shared_part = jnp.dot(shared_act, shared_down, preferred_element_type=F32)
    mine = lax.dynamic_slice_in_dim(shared_part, tp_index * part, part, 0)
    whole = lax.dynamic_update_slice_in_dim(
        shared_part, mine + resid + routed.astype(F32), tp_index * part, 0
    )
    added = lax.psum_scatter(whole, "tp", scatter_dimension=1, tiled=True)
    return added.astype(BF)


def solution(mesh):
    in_specs = (
        P("seq", None), P("seq"), P(), P(None, "tp"), P(None, "tp"), P(), P(None, "tp"),
        P(None, "tp"), P(), P("tp"), P("tp"), P("tp"), P("tp"), P("tp", None), P(), P(),
        P("seq", None), P("seq", None, None, "tp"), P("seq", "tp", None), P(None, None, "tp"),
        P("tp", None),
    )
    return jax.shard_map(
        body, mesh=mesh, in_specs=in_specs, out_specs=P("seq", "tp"), check_vma=False
    )
```

```python
import functools

import jax
import jax.numpy as jnp
from jax import lax
from jax.experimental import pallas as pl
from jax.experimental.pallas import tpu as pltpu
from jax.sharding import PartitionSpec as P

D = 1536
HEAD = 64
NSTATE = 128
LANES = 128
DI = 3072
epsilon = 1e-05
highest = lax.Precision.HIGHEST
F32 = jnp.float32
BF = jnp.bfloat16


def rms_apply(values, gain):
    mean_square = jnp.mean(values * values, axis=-1, keepdims=True)
    return values * lax.rsqrt(mean_square + epsilon) * gain.astype(F32)


def silu(v):
    return v / (1.0 + jnp.exp(-v))


MESH = pl.DeviceIdType.MESH


def mixer_kernel(
    heads, seqs, tps, x_ref, bc_ref, idc_ref, idr_ref, dt_ref, rate_ref, cx_ref, cb_ref, skip_ref,
    z_ref, gain_ref, out_ref, tok_ref, moe_gain_ref, router_ref, routes_ref, resid_ref, unit_ref,
    xs, bs, ids, tail, head_rows, ysum, slabs, got, back, entry, proj, sent, landed, sq_out, sq_in,
    tail_sems, go_sems, come_sems, ret_go, ret_come, tp_go, tp_come, sq_go, sq_come,
):
    me, mt = lax.axis_index("seq"), lax.axis_index("tp")
    n, width = x_ref.shape
    part = n // tps
    half_w = width // 2
    barrier = pltpu.get_barrier_semaphore()

    def greet(d, c):
        pl.semaphore_signal(
            barrier, inc=1, device_id={"seq": lax.rem(me + d, seqs)}, device_id_type=MESH
        )
        return c

    lax.fori_loop(1, seqs, greet, 0)
    for d in range(1, tps):
        pl.semaphore_signal(
            barrier, inc=1, device_id={"tp": lax.rem(mt + d, tps)}, device_id_type=MESH
        )
    xs[pl.ds(8, n), :] = x_ref[...].astype(F32)
    bs[pl.ds(8, n), :] = bc_ref[...].astype(F32)
    own = idc_ref[...]
    ids[pl.ds(8, n), :] = jnp.broadcast_to(own, (n, 128))
    tail[:, 0:width] = xs[pl.ds(n, 8), :]
    tail[:, width : width + 2 * NSTATE] = bs[pl.ds(n, 8), :]
    tail[:, width + 2 * NSTATE :] = ids[pl.ds(n, 8), :]
    pl.semaphore_wait(barrier, seqs - 1 + tps - 1)
    halo = pltpu.make_async_remote_copy(
        src_ref=tail, dst_ref=head_rows, send_sem=tail_sems.at[0], recv_sem=tail_sems.at[1],
        device_id={"seq": lax.rem(me + 1, seqs)}, device_id_type=MESH,
    )
    halo.start()

    raw = dt_ref[...]
    step = jnp.maximum(raw, 0.0) + jnp.log1p(jnp.exp(-jnp.abs(raw)))
    decay = -rate_ref[...] * step
    row = lax.broadcasted_iota(jnp.int32, (n, n), 0)
    col = lax.broadcasted_iota(jnp.int32, (n, n), 1)
    causal = row >= col
    tri = jnp.where(causal, 1.0, 0.0)
    cum = jnp.dot(tri, decay, precision=highest, preferred_element_type=F32)
    cum_t = cum.T
    last = cum[n - 1 : n, :]
    expand = jnp.where(
        lax.broadcasted_iota(jnp.int32, (128, width), 1) // HEAD
        == lax.broadcasted_iota(jnp.int32, (128, width), 0),
        1.0,
        0.0,
    )
    step_w = jnp.dot(step, expand, precision=highest, preferred_element_type=F32)
    at_end = own == idc_ref[n - 1 : n, :]
    to_end = jnp.where(at_end, jnp.exp(last - cum), 0.0)
    end_w = jnp.dot(to_end, expand, precision=highest, preferred_element_type=F32)
    carry_w = jnp.dot(jnp.exp(cum), expand, precision=highest, preferred_element_type=F32)
    r8 = lax.broadcasted_iota(jnp.int32, (NSTATE, 2 * NSTATE), 1)
    n8 = lax.broadcasted_iota(jnp.int32, (NSTATE, 2 * NSTATE), 0)
    same = n8 == 4 * (r8 // 8) + r8 % 4
    dup_l = jnp.where(same & (r8 % 8 < 4), 1.0, 0.0).astype(BF)
    dup_r = jnp.where(same & (r8 % 8 >= 4), 1.0, 0.0).astype(BF)
    dup = dup_l + dup_r
    low = lax.broadcasted_iota(jnp.int32, (2 * NSTATE, half_w), 0) % 8 < 4

    halo.wait()
    xs[pl.ds(0, 8), :] = head_rows[:, 0:width]
    bs[pl.ds(0, 8), :] = head_rows[:, width : width + 2 * NSTATE]
    ids[pl.ds(0, 8), :] = jnp.where(me == 0, -1.0, head_rows[:, width + 2 * NSTATE :])
    before_id = ids[pl.ds(7, 1), :]
    xsum = jnp.zeros((n, width), F32)
    bsum = jnp.zeros((n, 2 * NSTATE), F32)
    for k in range(4):
        live = ids[pl.ds(5 + k, n), 0:1] == own
        xsum += jnp.where(live, xs[pl.ds(5 + k, n), :], 0.0) * cx_ref[k : k + 1, :]
        bsum += jnp.where(live, bs[pl.ds(5 + k, n), :], 0.0) * cb_ref[k : k + 1, :]
    x_conv = silu(xsum).astype(BF).astype(F32)
    bc = silu(bsum).astype(BF)
    b_in, c_out = bc[:, :NSTATE], bc[:, NSTATE:]
    x_step = x_conv * step_w
    x_in = x_step.astype(BF)
    b_dup = jnp.dot(b_in, dup, preferred_element_type=F32).astype(BF)
    state = lax.dot_general(
        b_dup, (x_step * end_w).astype(BF), (((0,), (0,)), ((), ())), preferred_element_type=F32
    )
    state = jnp.where(low, state[:, :half_w], state[:, half_w:])
    slabs[:, :, 0:half_w] = state.reshape(seqs, 8, half_w)
    lane = lax.broadcasted_iota(jnp.int32, (1, 128), 1)
    note = jnp.where(lane == 127, idc_ref[n - 1 : n, :], last)
    slabs[:, :, half_w:] = jnp.broadcast_to(note[None], (seqs, 8, 128))

    def outward(d):
        peer = lax.rem(me + d, seqs)
        return pltpu.make_async_remote_copy(
            src_ref=slabs.at[peer], dst_ref=got.at[me], send_sem=go_sems.at[d],
            recv_sem=come_sems.at[d], device_id={"seq": peer}, device_id_type=MESH,
        )

    def homeward(d):
        peer = lax.rem(me + d, seqs)
        return pltpu.make_async_remote_copy(
            src_ref=back.at[peer], dst_ref=entry.at[me], send_sem=ret_go.at[d],
            recv_sem=ret_come.at[d], device_id={"seq": peer}, device_id_type=MESH,
        )

    def each(make, act):
        def one(d, c):
            getattr(make(d), act)()
            return c

        lax.fori_loop(1, seqs, one, 0)

    each(outward, "start")
    got[me] = slabs[me]

    scores = lax.dot_general(c_out, b_in, (((1,), (1,)), ((), ())), preferred_element_type=F32)
    scores = jnp.where(causal & (own == idr_ref[...]), scores, 0.0)

    def inner(pairs):
        half = n // 2
        for top, bottom in ((0, half), (half, n)):
            for pair in pairs:
                parts = []
                for h in (2 * pair, 2 * pair + 1):
                    diff = cum[top:bottom, h : h + 1] - cum_t[h : h + 1, :bottom]
                    mixing = scores[top:bottom, :bottom] * jnp.exp(jnp.minimum(diff, 0.0))
                    parts.append(
                        jnp.dot(
                            mixing.astype(BF), x_in[:bottom, h * HEAD : (h + 1) * HEAD],
                            preferred_element_type=F32,
                        )
                    )
                cols = slice(pair * 128, pair * 128 + 128)
                ysum[top:bottom, cols] = (
                    jnp.concatenate(parts, axis=1)
                    + x_conv[top:bottom, cols] * skip_ref[:, cols]
                )

    inner(range(0, heads // 4))
    each(outward, "wait")
    notes = got[:, :, half_w:].reshape(8 * seqs, 128)
    faded = jnp.dot(
        jnp.where(lax.broadcasted_iota(jnp.int32, notes.shape, 1) < heads, notes, 0.0),
        expand, precision=highest, preferred_element_type=F32,
    )
    faded = jnp.exp(jnp.where(low, faded[:, :half_w], faded[:, half_w:])).reshape(seqs, 8, half_w)
    ends = jnp.broadcast_to(notes[:, 127:128], (8 * seqs, half_w)).reshape(seqs, 8, half_w)
    running = jnp.zeros((8, half_w), F32)
    for q in range(seqs):
        back[q] = running
        if q == 0:
            running = got[q, :, 0:half_w]
        else:
            keep = jnp.where(ends[q] == ends[q - 1], faded[q], 0.0)
            running = running * keep + got[q, :, 0:half_w]
    each(homeward, "start")
    entry[me] = back[me]
    inner(range(heads // 4, heads // 2))
    c_l = jnp.dot(c_out, dup_l, preferred_element_type=F32).astype(BF)
    c_r = jnp.dot(c_out, dup_r, preferred_element_type=F32).astype(BF)
    zg = z_ref[...].astype(F32)
    gate = silu(zg)
    follows = own == before_id[:, 0:1]
    each(homeward, "wait")
    inc = entry[...].reshape(8 * seqs, half_w).astype(BF)
    before = jnp.concatenate(
        [
            jnp.dot(c_l, inc, preferred_element_type=F32),
            jnp.dot(c_r, inc, preferred_element_type=F32),
        ],
        axis=1,
    )
    scanned = ysum[...] + jnp.where(follows, before * carry_w, 0.0)
    gated = scanned * gate
    squares = jnp.sum(gated * gated, axis=1, keepdims=True)
    sq_out[...] = jnp.broadcast_to(squares, (n, 128)).reshape(tps, part, 128)
    lhs = (gated * gain_ref[...]).astype(BF)
    chunk = 512
    for c in range(D // chunk):
        cols = slice(c * chunk, (c + 1) * chunk)
        piece = jnp.dot(lhs, out_ref[:, cols], preferred_element_type=F32)
        piece = piece.reshape(tps, part, chunk)
        proj[:, :, cols] = piece
        sent[:, :, cols] = piece.astype(BF)
    moves = []
    for d in (2, 1, 3):
        peer = lax.rem(mt + d, tps)
        for src, dst, go, come in (
            (sent, landed, tp_go, tp_come),
            (sq_out, sq_in, sq_go, sq_come),
        ):
            move = pltpu.make_async_remote_copy(
                src_ref=src.at[peer], dst_ref=dst.at[d - 1], send_sem=go.at[d - 1],
                recv_sem=come.at[d - 1], device_id={"tp": peer}, device_id_type=MESH,
            )
            move.start()
            moves.append(move)
    total = proj[mt]
    sq = sq_out[mt]
    for move in moves:
        move.wait()
    for d in range(tps - 1):
        total = total + landed[d].astype(F32)
        sq = sq + sq_in[d]
    resid = tok_ref[...].astype(F32) + total * lax.rsqrt(sq[:, 0:1] / DI + epsilon)
    resid_ref[...] = resid
    power = jnp.sum(resid * resid, axis=1, keepdims=True) / D
    moe_in = (resid * lax.rsqrt(power + epsilon) * moe_gain_ref[...]).astype(BF)
    unit_ref[:, 0:D] = moe_in
    logits = jnp.dot(moe_in, router_ref[...], preferred_element_type=F32)
    expert = lax.broadcasted_iota(jnp.int32, logits.shape, 1)
    named = expert == routes_ref[:, 0:1]
    for k in range(1, routes_ref.shape[1]):
        named = named | (expert == routes_ref[:, k : k + 1])
    sigmas = jnp.where(named, 1.0 / (1.0 + jnp.exp(-logits)), 0.0)
    wts = sigmas / jnp.sum(sigmas, axis=1, keepdims=True)
    unit_ref[:, D:] = jnp.concatenate(
        [wts, jnp.zeros((part, LANES - wts.shape[1]), F32)], axis=1
    ).astype(BF)


def mixer(seqs, tps, heads, *args):
    n, width = args[0].shape
    part = n // tps
    vm = pl.BlockSpec(memory_space=pltpu.VMEM)
    dma = pltpu.SemaphoreType.DMA
    return pl.pallas_call(
        functools.partial(mixer_kernel, heads, seqs, tps),
        out_shape=(
            jax.ShapeDtypeStruct((part, D), F32),
            jax.ShapeDtypeStruct((part, D + LANES), BF),
        ),
        in_specs=[vm] * len(args),
        out_specs=(vm, vm),
        scratch_shapes=[
            pltpu.VMEM((n + 8, width), F32),
            pltpu.VMEM((n + 8, 2 * NSTATE), F32),
            pltpu.VMEM((n + 8, 128), F32),
            pltpu.VMEM((8, width + 2 * NSTATE + 128), F32),
            pltpu.VMEM((8, width + 2 * NSTATE + 128), F32),
            pltpu.VMEM((n, width), F32),
            pltpu.VMEM((seqs, 8, width // 2 + 128), F32),
            pltpu.VMEM((seqs, 8, width // 2 + 128), F32),
            pltpu.VMEM((seqs, 8, width // 2), F32),
            pltpu.VMEM((seqs, 8, width // 2), F32),
            pltpu.VMEM((tps, part, D), F32),
            pltpu.VMEM((tps, part, D), BF),
            pltpu.VMEM((tps - 1, part, D), BF),
            pltpu.VMEM((tps, part, 128), F32),
            pltpu.VMEM((tps - 1, part, 128), F32),
            dma((2,)),
            dma((seqs,)),
            dma((seqs,)),
            dma((seqs,)),
            dma((seqs,)),
            dma((tps - 1,)),
            dma((tps - 1,)),
            dma((tps - 1,)),
            dma((tps - 1,)),
        ],
        compiler_params=pltpu.CompilerParams(collective_id=0, has_side_effects=True),
        name="mixer",
    )(*args)


NX, NY, NC = 4, 4, 2


def moe_kernel(
    tps, unit, resid, gu_own, gu_left, gu_right, dn_own, dn_left, dn_right, sgu, sdn, out,
    plane, line, gu, dn, away, partner, sums, b_in, a_in, b2_in, a2_in, sh_out, sh_in, fin_out,
    fin_in, acc, send, recv, tp_send, tp_recv, far_send, far_recv, load_sem, core_send, core_recv,
):
    me, mt = lax.axis_index("seq"), lax.axis_index("tp")
    c, x, y = lax.rem(me, NC), lax.rem(me // NC, NX), me // (NC * NX)
    rows = unit.shape[0]
    experts, wide = gu_own.shape[0], gu_own.shape[3]
    half, quarter = rows // 2, rows // 4
    count = [0]

    def wrap(v, n):
        return lax.rem(v + n, n)

    def near(d, s):
        if d == "x":
            return (y * NX + wrap(x + s, NX)) * NC + c
        if d == "y":
            return (wrap(y + s, NY) * NX + x) * NC + c
        return (y * NX + x) * NC + (1 - c)

    def send_to(src, dst, dev):
        i = count[0]
        count[0] += 1
        move = pltpu.make_async_remote_copy(
            src_ref=src, dst_ref=dst, send_sem=send.at[i], recv_sem=recv.at[i],
            device_id={"seq": dev}, device_id_type=MESH,
        )
        move.start()
        return move

    barrier = pltpu.get_barrier_semaphore()
    for d, s in (("x", 1), ("x", -1), ("y", 1), ("y", -1), ("c", 1)):
        pl.semaphore_signal(barrier, inc=1, device_id={"seq": near(d, s)}, device_id_type=MESH)
    for d in range(1, tps):
        pl.semaphore_signal(
            barrier, inc=1, device_id={"tp": lax.rem(mt + d, tps)}, device_id_type=MESH
        )
    loads = []

    def load(src, dst):
        copy = pltpu.make_async_copy(src, dst, load_sem.at[len(loads)])
        copy.start()
        loads.append(copy)

    def columns(k, slot):
        return pl.ds((k * tps + slot) * wide, wide)

    for slot, (g, w) in enumerate(((gu_own, dn_own), (gu_left, dn_left), (gu_right, dn_right))):
        for e in range(experts):
            for k in range(2):
                load(g.at[e, k], gu.at[e, :, columns(k, slot)])
            load(w.at[e], dn.at[e, pl.ds(slot * wide, wide), :])
    plane[y, x, c] = unit[...]
    pl.semaphore_wait(barrier, 5 + tps - 1)

    later = []

    def place(d1, o1, d2, o2):
        off = {d1: o1, d2: o2}
        return plane.at[wrap(y + off["y"], NY), wrap(x + off["x"], NX), c]

    plans = (("y", "x", 0), ("x", "y", half))
    own_rows = [unit.at[pl.ds(r0, half)] for _, _, r0 in plans]

    def block(p, o1, o2, start=0, size=half):
        d1, d2, r0 = plans[p]
        return place(d1, o1, d2, o2).at[pl.ds(r0 + start, size)]

    def share(p, o1, o2):
        later.append(
            send_to(own_rows[p] if (o1, o2) == (0, 0) else block(p, o1, o2), block(p, o1, o2),
                    near("c", 1))
        )

    first, second, relay, relay2 = {}, {}, {}, {}
    for p in (0, 1):
        d1, d2, _ = plans[p]
        for s in (1, -1):
            first[p, s] = send_to(own_rows[p], block(p, 0, 0), near(d1, s))
    for d in (2, 1, 3):
        peer = lax.rem(mt + d, tps)
        move = pltpu.make_async_remote_copy(
            src_ref=unit, dst_ref=line.at[d - 1], send_sem=tp_send.at[d - 1],
            recv_sem=tp_recv.at[d - 1], device_id={"tp": peer}, device_id_type=MESH,
        )
        move.start()
        later.append(move)
    lines = later[-(tps - 1) :]
    far = []
    for e, s, g, w in ((0, 1, gu_left, dn_left), (1, tps - 1, gu_right, dn_right)):
        pieces = [(g.at[e, k], gu.at[e, :, columns(k, tps - 1)]) for k in range(2)]
        pieces.append((w.at[e], dn.at[e, pl.ds((tps - 1) * wide, wide), :]))
        for src, dst in pieces:
            move = pltpu.make_async_remote_copy(
                src_ref=src, dst_ref=dst, send_sem=far_send.at[len(far)],
                recv_sem=far_recv.at[len(far)], device_id={"tp": lax.rem(mt + s, tps)},
                device_id_type=MESH,
            )
            move.start()
            far.append(move)
    for p in (0, 1):
        d1, d2, _ = plans[p]
        for s in (1, -1):
            second[p, 0, s] = send_to(own_rows[p], block(p, 0, 0), near(d2, s))
        share(p, 0, 0)
    for s, start in ((1, 0), (-1, quarter)):
        for p in (0, 1):
            d1, d2, _ = plans[p]
            first[p, s].wait_recv()
            piece = block(p, -s, 0, start, quarter)
            relay[p, s] = send_to(piece, piece, near(d1, s))
            for t in (1, -1):
                second[p, -s, t] = send_to(block(p, -s, 0), block(p, -s, 0), near(d2, t))
            share(p, -s, 0)
    for p in (0, 1):
        d1, d2, _ = plans[p]
        relay[p, 1].wait_recv()
        relay[p, -1].wait_recv()
        for t in (1, -1):
            second[p, 2, t] = send_to(block(p, 2, 0), block(p, 2, 0), near(d2, t))
        share(p, 2, 0)
    for o in (0, -1, 1, 2):
        for s, start in ((1, 0), (-1, quarter)):
            for p in (0, 1):
                d1, d2, _ = plans[p]
                second[p, o, s].wait_recv()
                piece = block(p, o, -s, start, quarter)
                relay2[p, o, s] = send_to(piece, piece, near(d2, s))
                share(p, o, -s)

    for move in lines:
        move.wait_recv()
    rows_in = jnp.concatenate(
        [unit[:, 0:D]] + [line[d, :, 0:D] for d in range(tps - 1)], axis=0
    )
    hidden = silu(jnp.dot(rows_in, sgu[0], preferred_element_type=F32)) * jnp.dot(
        rows_in, sgu[1], preferred_element_type=F32
    )
    hidden = hidden.astype(BF)
    cut = D // tps
    for b in range(tps):
        piece = jnp.dot(
            hidden, sdn[:, b * cut : (b + 1) * cut], preferred_element_type=F32
        )
        for j in range(tps):
            some = piece[j * rows : (j + 1) * rows]
            if j == 0:
                some = some + resid[:, b * cut : (b + 1) * cut]
            sh_out[b, wrap(mt - j, tps)] = some.astype(BF)
    spread = []

    def to_line(src, dst, k, i):
        peer = lax.rem(mt + k, tps)
        move = pltpu.make_async_remote_copy(
            src_ref=src.at[peer], dst_ref=dst.at[k - 1], send_sem=tp_send.at[i],
            recv_sem=tp_recv.at[i], device_id={"tp": peer}, device_id_type=MESH,
        )
        move.start()
        return move

    for k in (2, 1, 3):
        spread.append(to_line(sh_out, sh_in, k, tps - 1 + k - 1))
    for o in (0, -1, 1, 2):
        for p in (0, 1):
            relay2[p, o, 1].wait_recv()
            relay2[p, o, -1].wait_recv()
            share(p, o, 2)
    for copy in loads:
        copy.wait()
    for move in far:
        move.wait()
    for move in list(first.values()) + list(second.values()):
        move.wait_send()
    for move in list(relay.values()) + list(relay2.values()):
        move.wait_send()
    for move in later:
        if not any(move is m for m in lines):
            move.wait()
    for move in lines:
        move.wait_send()

    width = tps * wide
    tile_rows = NY * rows

    def expert_tile(xi, ci):
        block_in = plane[:, xi, ci].reshape(tile_rows, D + LANES)
        data = block_in[:, 0:D]
        names = block_in[:, D:].astype(F32)
        lane = lax.broadcasted_iota(jnp.int32, names.shape, 1)
        total = None
        for e in range(experts):
            wt = jnp.sum(jnp.where(lane == me * experts + e, names, 0.0), axis=1, keepdims=True)
            both = jnp.dot(data, gu[e], preferred_element_type=F32)
            act = (silu(both[:, :width]) * both[:, width:] * wt).astype(BF)
            part = jnp.dot(act, dn[e], preferred_element_type=F32)
            total = part if total is None else total + part
        return total.reshape(NY, rows, D)

    def core_move(i):
        xi = wrap(x + 2 - i, NX)
        return pltpu.make_async_remote_copy(
            src_ref=away.at[:, xi], dst_ref=partner.at[:, xi], send_sem=core_send.at[i],
            recv_sem=core_recv.at[i], device_id={"seq": near("c", 1)}, device_id_type=MESH,
        )

    def partner_tile(i, carry):
        xi = wrap(x + 2 - i, NX)
        away[:, xi] = expert_tile(xi, 1 - c).astype(BF)
        core_move(i).start()
        return carry

    lax.fori_loop(0, NX, partner_tile, 0)

    def own_tile(i, carry):
        xi = wrap(x + 2 - i, NX)
        total = expert_tile(xi, c)
        core_move(i).wait()
        sums[:, xi] = (total + partner[:, xi].astype(F32)).astype(BF)
        return carry

    lax.fori_loop(0, NX, own_tile, 0)

    plans = (("x", "y", 0), ("y", "x", half))

    def row_line(d, o, r0, size):
        if d == "x":
            return sums.at[:, wrap(x + o, NX), pl.ds(r0, size)]
        return sums.at[wrap(y + o, NY), :, pl.ds(r0, size)]

    def cell(d, o, r0, size):
        if d == "x":
            return sums.at[y, wrap(x + o, NX), pl.ds(r0, size)]
        return sums.at[wrap(y + o, NY), x, pl.ds(r0, size)]

    def add(ref, *others):
        value = ref[...].astype(F32)
        for other in others:
            value = value + other[...].astype(F32)
        ref[...] = value.astype(BF)

    done = []
    final = [None, None]

    def reduce_stage(pick, which, b_buf, a_buf, last):
        bs_, as_ = {}, {}
        for p in (0, 1):
            d, r0 = plans[p][which], plans[p][2]
            bs_[p, 0] = send_to(pick(d, 2, r0, quarter), b_buf.at[p, 0], near(d, 1))
            bs_[p, 1] = send_to(pick(d, 2, r0 + quarter, quarter), b_buf.at[p, 1], near(d, -1))
        for p in (0, 1):
            d, r0 = plans[p][which], plans[p][2]
            bs_[p, 0].wait_recv()
            add(pick(d, 1, r0, quarter), b_buf.at[p, 0])
            as_[p, 0] = send_to(pick(d, 1, r0, half), a_buf.at[p, 0], near(d, 1))
            bs_[p, 1].wait_recv()
            add(pick(d, -1, r0 + quarter, quarter), b_buf.at[p, 1])
            as_[p, 1] = send_to(pick(d, -1, r0, half), a_buf.at[p, 1], near(d, -1))
        for p in (0, 1):
            d, r0 = plans[p][which], plans[p][2]
            as_[p, 0].wait_recv()
            as_[p, 1].wait_recv()
            if last:
                final[p] = (
                    pick(d, 0, r0, half)[...].astype(F32)
                    + a_buf[p, 0].astype(F32)
                    + a_buf[p, 1].astype(F32)
                )
            else:
                add(pick(d, 0, r0, half), a_buf.at[p, 0], a_buf.at[p, 1])
        done.extend(bs_.values())
        done.extend(as_.values())

    reduce_stage(row_line, 0, b_in, a_in, False)
    reduce_stage(cell, 1, b2_in, a2_in, True)
    routed = jnp.concatenate(final, axis=0)
    for b in range(tps):
        fin_out[b] = routed[:, b * cut : (b + 1) * cut].astype(BF)
    last = [to_line(fin_out, fin_in, k, 2 * (tps - 1) + k - 1) for k in (2, 1, 3)]
    for move in spread:
        move.wait()
    total = sh_out[mt].astype(F32)
    for k in range(tps - 1):
        total = total + sh_in[k].astype(F32)
    acc[...] = total
    acc[mt] += fin_out[mt].astype(F32)
    for move in last:
        move.wait()
    for k in range(1, tps):
        acc[wrap(mt - k, tps)] += fin_in[k - 1].astype(F32)
    for move in done:
        move.wait_send()
    out[...] = acc[...].reshape(tps * rows, cut).astype(BF)


def experts(tps, unit, resid, gus, dns, shared_gate_up, shared_down):
    rows = unit.shape[0]
    count, _, _, wide = gus[0].shape
    cut = D // tps
    half, quarter = rows // 2, rows // 4
    vm = pl.BlockSpec(memory_space=pltpu.VMEM)
    hbm = pl.BlockSpec(memory_space=pl.ANY)
    dma = pltpu.SemaphoreType.DMA
    return pl.pallas_call(
        functools.partial(moe_kernel, tps),
        out_shape=jax.ShapeDtypeStruct((tps * rows, cut), BF),
        in_specs=[vm, vm] + [hbm] * 6 + [vm, vm],
        out_specs=vm,
        scratch_shapes=[
            pltpu.VMEM((NY, NX, NC, rows, D + LANES), BF),
            pltpu.VMEM((tps - 1, rows, D + LANES), BF),
            pltpu.VMEM((count, D, 2 * tps * wide), BF),
            pltpu.VMEM((count, tps * wide, D), BF),
            pltpu.VMEM((NY, NX, rows, D), BF),
            pltpu.VMEM((NY, NX, rows, D), BF),
            pltpu.VMEM((NY, NX, rows, D), BF),
            pltpu.VMEM((2, 2, NX, quarter, D), BF),
            pltpu.VMEM((2, 2, NX, half, D), BF),
            pltpu.VMEM((2, 2, quarter, D), BF),
            pltpu.VMEM((2, 2, half, D), BF),
            pltpu.VMEM((tps, tps, rows, cut), BF),
            pltpu.VMEM((tps - 1, tps, rows, cut), BF),
            pltpu.VMEM((tps, rows, cut), BF),
            pltpu.VMEM((tps - 1, rows, cut), BF),
            pltpu.VMEM((tps, rows, cut), F32),
            dma((96,)),
            dma((96,)),
            dma((3 * (tps - 1),)),
            dma((3 * (tps - 1),)),
            dma((3 * count,)),
            dma((3 * count,)),
            dma((9 * count,)),
            dma((NX,)),
            dma((NX,)),
        ],
        compiler_params=pltpu.CompilerParams(
            collective_id=1, has_side_effects=True, vmem_limit_bytes=60 << 20
        ),
        name="experts",
    )(unit, resid, *gus, *dns, shared_gate_up, shared_down)


def body(
    tokens, doc_ids, mix_gain, zgate_proj, xin_proj, bc_proj, dt_proj, conv_x, conv_bc, dt_bias,
    decay_rate, skip_gain, norm_gain, out_proj, moe_gain, router, routes, expert_gate_up,
    expert_down, shared_gate_up, shared_down,
):
    rows = tokens.shape[0]
    tp_index = lax.axis_index("tp")
    tp_count, seq_count = lax.axis_size("tp"), lax.axis_size("seq")
    heads = dt_proj.shape[1]
    part = rows // tp_count

    def shift(value, steps):
        pairs = [(t, (t + steps) % tp_count) for t in range(tp_count)]
        return lax.ppermute(value, "tp", pairs)

    gu_left, dn_left = shift(expert_gate_up, 1), shift(expert_down, 1)
    gu_right, dn_right = shift(expert_gate_up, -1), shift(expert_down, -1)
    own_routes = lax.dynamic_slice_in_dim(routes, tp_index * part, part, 0)
    resid_in = tokens.astype(F32)
    normed_in = rms_apply(resid_in, mix_gain).astype(BF)
    zgate = jnp.dot(normed_in, zgate_proj, preferred_element_type=F32).astype(BF)
    x_pre = jnp.dot(normed_in, xin_proj, preferred_element_type=F32).astype(BF)
    bc_pre = jnp.dot(normed_in, bc_proj, preferred_element_type=F32).astype(BF)
    dt_raw = jnp.dot(normed_in, dt_proj, preferred_element_type=F32) + dt_bias
    dt_raw = jnp.pad(dt_raw, ((0, 0), (0, 128 - heads)))
    rate = jnp.pad(decay_rate, (0, 128 - heads))[None, :]
    own_rows = lax.dynamic_slice_in_dim(tokens, tp_index * part, part, 0)
    ids = doc_ids.astype(F32)
    resid, unit = mixer(
        seq_count, tp_count, heads, x_pre, bc_pre, ids[:, None], ids[None, :], dt_raw, rate,
        conv_x.astype(F32), conv_bc.astype(F32), jnp.repeat(skip_gain, HEAD)[None, :], zgate,
        norm_gain.astype(F32)[None, :], out_proj, own_rows, moe_gain.astype(F32)[None, :],
        router, own_routes,
    )
    return experts(
        tp_count, unit, resid, (expert_gate_up, gu_left, gu_right),
        (expert_down, dn_left, dn_right), shared_gate_up, shared_down,
    )


def solution(mesh):
    in_specs = (
        P("seq", None), P("seq"), P(), P(None, "tp"), P(None, "tp"), P(), P(None, "tp"),
        P(None, "tp"), P(), P("tp"), P("tp"), P("tp"), P("tp"), P("tp", None), P(), P(),
        P("seq", None), P("seq", None, None, "tp"), P("seq", "tp", None), P(None, None, "tp"),
        P("tp", None),
    )
    return jax.shard_map(
        body, mesh=mesh, in_specs=in_specs, out_specs=P("seq", "tp"), check_vma=False
    )
```
